32 devices in a mesh: dp: 4 (over z), cent: 8 (over y, x, core).
Axes of the slice: x: 2, y: 2, z: 4, core: 2. Of those that a mesh axis runs over, the one named last changes fastest.
Arguments:
- vectors: bfloat16 [1024, 1024], P(('dp', 'cent')), may hold values from -18 to 18
- centroids: bfloat16 [16384, 1024], P('cent'), may hold values from -18 to 18
- primary: int32 [1024], P(('dp', 'cent')), may hold values from 0 to 16383, as said below
- secondary: int32 [1024], P(('dp', 'cent')), may hold values from 0 to 16383, as said below
Outputs:
- soft_cost: float32 [1024], P(('dp', 'cent'))
- list_sums: bfloat16 [16384, 1024], P('cent', 'dp')
The draws below stay inside these ranges and needn't reach their ends.
Inputs may be any that keep to these rules, and one draw needn't show every extreme that they name: In each device's aligned block of 32 vectors at most 8 primary ids fall in one range of 2048 centroids (ids with equal id // 2048); in each dp group of 256 vectors one range receives exactly 8 from every block of the group. Secondary ids obey the same bound per block and range, and in each dp group the range that is full for primary ids is full for secondary ids too.
All inputs are finite; a program needn't handle non-finite values.
Results may differ from the reference program's by a relative error of at most 0.001.
Values may be sent and summed in bfloat16 or wider, within the bound.
No kernel may reach another device: no remote copies, remote signals or barrier semaphores. Data moves between devices by JAX's collectives and lax.ppermute only.
A program may use at most 64 MiB of HBM per device.

```python
import math
import jax
import jax.numpy as jnp
from jax import lax

D = 1024
K_DEV = 2048
ROW_DEV = 32
CENT = 16384
VECTORS = 1024
CAP = 8
N_CENT = 8


def loud_offset(key):
    return jax.random.randint(jax.random.fold_in(key, 505), (), 0, 32)


def centroid_row(key, index):
    pair = index // 2
    pair_key = jax.random.fold_in(jax.random.fold_in(key, 501), pair)
    odd_part = (index % 2).astype(jnp.float32)
    loud = (pair + loud_offset(key)) % 32 == 0
    strength = jnp.exp(jax.random.uniform(jax.random.fold_in(pair_key, 11), (), jnp.float32, math.log(6.0), math.log(16.0)))
    loud_signs = jnp.where(jax.random.bernoulli(jax.random.fold_in(pair_key, 12), 0.5, (D,)), 1.0, -1.0)
    loud_base = loud_signs * strength * jax.random.uniform(jax.random.fold_in(pair_key, 13), (D,), jnp.float32, 0.8, 1.0)
    delta_signs = jnp.where(jax.random.bernoulli(jax.random.fold_in(pair_key, 14), 0.5, (D,)), 1.0, -1.0)
    loud_delta = delta_signs * math.sqrt(80.0 / D) * jax.random.uniform(jax.random.fold_in(pair_key, 15), (D,), jnp.float32, 0.5, 1.5)
    loud_row = loud_base + loud_delta * odd_part
    drawn_row = jax.random.truncated_normal(jax.random.fold_in(jax.random.fold_in(key, 503), index), -4.0, 4.0, (D,), jnp.float32)
    return jnp.where(loud, loud_row, drawn_row)


def draw_centroids(key, part):

    def one_row(index):
        return centroid_row(key, index)
    return jax.vmap(one_row)(jnp.arange(CENT, dtype=jnp.int32)).astype(jnp.bfloat16)


def draw_vectors(key, part):
    drawn = jax.random.truncated_normal(jax.random.fold_in(key, 605), -4.0, 4.0, (VECTORS, D), jnp.float32)
    aligned = jax.random.randint(jax.random.fold_in(key, 603), (VECTORS,), 0, 16) == 0
    loud_pick = jax.random.randint(jax.random.fold_in(key, 604), (VECTORS,), 0, CENT // 64)
    target_pair = loud_pick * 32 + (32 - loud_offset(key)) % 32
    target = (2 * target_pair).astype(jnp.int32)

    def one_row(index):
        return centroid_row(key, index)
    matched = jax.vmap(one_row)(target)
    rows = jnp.where(aligned[:, None], matched, drawn)
    return rows.astype(jnp.bfloat16)


def owner_pattern(key, salt):
    block_total = VECTORS // ROW_DEV

    def one_block(block):
        group_index = block // N_CENT
        hot_owner = jax.random.randint(jax.random.fold_in(jax.random.fold_in(key, 701), group_index), (), 0, N_CENT)
        block_key = jax.random.fold_in(jax.random.fold_in(key, salt), block)
        owner_pool = jnp.arange((N_CENT - 1) * CAP, dtype=jnp.int32) // CAP
        owner_pool = owner_pool + (owner_pool >= hot_owner).astype(jnp.int32)
        mixed = jax.random.permutation(jax.random.fold_in(block_key, 1), owner_pool)[:ROW_DEV - CAP]
        owners = jnp.concatenate([jnp.full((CAP,), hot_owner, jnp.int32), mixed])
        owners = jax.random.permutation(jax.random.fold_in(block_key, 2), owners)
        local_ids = jax.random.randint(jax.random.fold_in(block_key, 3), (ROW_DEV,), 0, K_DEV)
        return owners * K_DEV + local_ids
    return jax.vmap(one_block)(jnp.arange(block_total, dtype=jnp.int32)).reshape(VECTORS).astype(jnp.int32)


def draw_primary(key, part):
    return owner_pattern(key, 711)


def draw_secondary(key, part):
    return owner_pattern(key, 713)


def setup_inputs(seed: int = 0) -> dict:
    keys = jax.random.split(jax.random.key(seed), 5)
    vectors = draw_vectors(jax.random.fold_in(keys[4], 71), 0)
    centroids = draw_centroids(jax.random.fold_in(keys[4], 71), 0)
    primary = draw_primary(jax.random.fold_in(keys[4], 71), 0)
    secondary = draw_secondary(jax.random.fold_in(keys[4], 71), 0)
    return dict(vectors=vectors, centroids=centroids, primary=primary, secondary=secondary)


perpendicular_weighting = 1.5
logit_divisor = 40.0
spill_offset = 2.0


def score_block(packed, centroids, center_length_squared):
    block_x, block_r, block_sec = packed
    x_float = block_x.astype(jnp.float32)
    r_float = block_r.astype(jnp.float32)
    leftover_dot_point = jnp.sum(r_float * x_float, axis=1)
    logit_range_gap = jnp.mean(r_float * r_float, axis=1) + 1e-5
    point_dot_center = jnp.dot(block_x, centroids.T, preferred_element_type=jnp.float32)
    leftover_dot_center = jnp.dot(block_r, centroids.T, preferred_element_type=jnp.float32)
    feature_dimension = block_x.shape[1]
    normalized_exponent_likelihood = (2.0 * point_dot_center - center_length_squared[None, :] - perpendicular_weighting * (leftover_dot_point[:, None] - leftover_dot_center) ** 2 / (feature_dimension * logit_range_gap[:, None])) / logit_divisor
    row_top = jnp.max(normalized_exponent_likelihood, axis=1)
    lse = row_top + jnp.log(jnp.sum(jnp.exp(normalized_exponent_likelihood - row_top[:, None]), axis=1))
    picked = jnp.take_along_axis(normalized_exponent_likelihood, block_sec[:, None].astype(jnp.int32), axis=1)[:, 0]
    return lse, picked


def reference(vectors, centroids, primary, secondary):
    cent_float = centroids.astype(jnp.float32)
    center_length_squared = jnp.sum(cent_float * cent_float, axis=1)
    primary_rows = centroids[primary]
    residual = (vectors.astype(jnp.float32) - primary_rows.astype(jnp.float32)).astype(jnp.bfloat16)
    block_rows = 256
    block_count = vectors.shape[0] // block_rows
    feature_dimension = vectors.shape[1]
    packed = (vectors.reshape(block_count, block_rows, feature_dimension), residual.reshape(block_count, block_rows, feature_dimension), secondary.reshape(block_count, block_rows))
    lse, picked = lax.map(lambda item: score_block(item, centroids, center_length_squared), packed)
    lse = lse.reshape(-1)
    picked = picked.reshape(-1)
    log_count = math.log(CENT)
    soft_cost = lse - log_count
    spill_weight = jax.nn.sigmoid(picked - lse + log_count + spill_offset)
    x_float = vectors.astype(jnp.float32)
    list_total = jnp.zeros((CENT, feature_dimension), jnp.float32)
    list_total = list_total.at[primary].add(x_float - cent_float[primary])
    list_total = list_total.at[secondary].add(spill_weight[:, None] * (x_float - cent_float[secondary]))
    return soft_cost, list_total.astype(jnp.bfloat16)
```

```python
import functools
import math

import jax
import jax.numpy as jnp
from jax import lax
from jax.experimental import pallas as pl
from jax.experimental.pallas import tpu as pltpu
from jax.sharding import PartitionSpec as P

perpendicular_weighting = 1.5
logit_divisor = 40.0
spill_offset = 2.0
BF = jnp.bfloat16
F32 = jnp.float32
I32 = jnp.int32
META = 8
VMEM_LIMIT = 24 * 1024 * 1024


def iota(shape, dim):
    return lax.broadcasted_iota(I32, shape, dim)


def nn(a, b):
    return lax.dot_general(a, b, (((1,), (0,)), ((), ())), preferred_element_type=F32)


def nt(a, b):
    return lax.dot_general(a, b, (((1,), (1,)), ((), ())), preferred_element_type=F32)


def as_bf(mask):
    return jnp.where(mask, 1.0, 0.0).astype(BF)


def call(kernel, outs, args, flops=0, nbytes=0, scratch=(), smem=0, limit=VMEM_LIMIT):
    specs = [pl.BlockSpec(memory_space=pltpu.SMEM)] * smem
    specs += [pl.BlockSpec(memory_space=pltpu.VMEM)] * (len(args) - smem)
    return pl.pallas_call(
        kernel,
        out_shape=tuple(jax.ShapeDtypeStruct(s, t) for s, t in outs),
        in_specs=specs,
        out_specs=tuple(pl.BlockSpec(memory_space=pltpu.VMEM) for _ in outs),
        scratch_shapes=list(scratch),
        compiler_params=pltpu.CompilerParams(vmem_limit_bytes=limit),
        cost_estimate=pl.CostEstimate(flops=flops, bytes_accessed=nbytes, transcendentals=0),
    )(*args)


def pack_kernel(x_ref, prim_ref, sec_ref, out_ref):
    rows = x_ref.shape[0]
    out_ref[0:rows, :] = x_ref[...]
    out_ref[rows:, 0:128] = jnp.zeros((META, 128), BF)
    for q, ref in ((0, prim_ref), (2, sec_ref)):
        ids = ref[...]
        out_ref[rows + q : rows + q + 1, 0:rows] = (ids >> 8).astype(F32).astype(BF)
        out_ref[rows + q + 1 : rows + q + 2, 0:rows] = (ids & 255).astype(F32).astype(BF)


def rows_kernel(rows, cap, parts, shift, me_ref, *refs):
    blocks = refs[:parts]
    cent_ref, info_ref, out_ref = refs[parts:]
    group = rows * parts
    me = me_ref[0]
    spread = as_bf(iota((128, group), 0) == (iota((128, group), 1) % rows))
    lane_block = iota((META, group), 1) // rows
    bytes8 = jnp.zeros((META, group), F32)
    for s, ref in enumerate(blocks):
        got = nn(ref[rows : rows + META, 0:128], spread)
        bytes8 = bytes8 + jnp.where(lane_block == (me ^ s), got, 0.0)
    bytes8 = bytes8.astype(I32)
    prim = bytes8[0:1] * 256 + bytes8[1:2]
    sec = bytes8[2:3] * 256 + bytes8[3:4]
    before = (iota((group, group), 0) < iota((group, group), 1)) & (
        iota((group, group), 0) // rows == iota((group, group), 1) // rows
    )
    before = as_bf(before)
    ranks = []
    for ids in (prim, sec):
        same = iota((parts, group), 0) == (ids >> shift)
        count = nn(as_bf(same), before)
        ranks.append(jnp.sum(jnp.where(same, count, 0.0), axis=0, keepdims=True).astype(I32))
    base = (iota((1, group), 1) // rows) * cap
    slot_p = base + ranks[0]
    slot_s = base + ranks[1]
    info_ref[0:1, :] = prim
    info_ref[1:2, :] = sec
    info_ref[2:3, :] = slot_p
    info_ref[3:4, :] = slot_s
    info_ref[4:8, :] = jnp.zeros((4, group), I32)
    slots = cap * parts
    keep = (iota((slots, group), 0) == slot_p) & ((prim >> shift) == me)
    local = jnp.where(keep, (prim & ((1 << shift) - 1)) + 1, 0).astype(F32)
    row_id = jnp.sum(local, axis=1, keepdims=True).astype(I32) - 1
    pick = as_bf(iota((slots, 1 << shift), 1) == row_id)
    out_ref[...] = nn(pick, cent_ref[...]).astype(BF)


def slots_kernel(rows, cap, parts, dps, shift, me_ref, *refs):
    blocks = refs[:parts]
    info_ref, x_ref = refs[parts : parts + 2]
    outs = refs[parts + 2 : parts + 2 + dps]
    picked_ref = refs[-1]
    group = rows * parts
    slots = cap * parts
    me = me_ref[0]
    me_dp = me_ref[1]
    for s, ref in enumerate(blocks):
        at = pl.multiple_of((me ^ s) * rows, rows)
        x_ref[pl.ds(at, rows), :] = ref[0:rows, :]
    prim, sec = info_ref[0:1, :], info_ref[1:2, :]
    slot_p, slot_s = info_ref[2:3, :], info_ref[3:4, :]
    keep_p = (iota((slots, group), 0) == slot_p) & ((prim >> shift) == me)
    keep_s = (iota((slots, group), 0) == slot_s) & ((sec >> shift) == me)
    pick = jnp.concatenate([as_bf(keep_p), as_bf(keep_s)], axis=0)
    picked_ref[...] = nn(pick, x_ref[...]).astype(BF)
    where = iota((1, group), 1)
    meta = jnp.concatenate(
        [
            jnp.ones((1, group), F32),
            (where >> 8).astype(F32),
            (where & 255).astype(F32),
            jnp.zeros((5, group), F32),
        ],
        axis=0,
    ).astype(BF)
    mask = (1 << shift) - 1
    local_p, local_s = prim & mask, sec & mask
    loc = jnp.concatenate(
        [
            (local_p >> 8).astype(F32),
            (local_p & 255).astype(F32),
            (local_s >> 8).astype(F32),
            (local_s & 255).astype(F32),
            jnp.zeros((4, group), F32),
        ],
        axis=0,
    ).astype(BF)
    facts = jnp.concatenate([nt(meta, pick), nt(loc, pick)], axis=0).astype(BF)
    width = x_ref.shape[1] // dps
    for s in range(dps):
        at = pl.multiple_of((me_dp ^ s) * width, width)
        outs[s][0 : 2 * slots, :] = picked_ref[:, pl.ds(at, width)]
        outs[s][2 * slots :, 0:128] = facts


def base_kernel(tile, x_ref, cent_ref, out_ref):
    x = x_ref[...]

    @pl.loop(0, cent_ref.shape[0], step=tile)
    def _(k):
        k = pl.multiple_of(k, tile)
        c = cent_ref[pl.ds(k, tile), :]
        cf = c.astype(F32)
        norm = jnp.sum(cf * cf, axis=1, keepdims=True)
        out_ref[pl.ds(k, tile), :] = 2.0 * nt(c, x) - norm


def score_kernel(rows, cap, parts, shift, tile, me_ref, *refs):
    owned = refs[:parts]
    x_ref, info_ref, cent_ref, base_ref, out_ref, r_ref, t_ref = refs[parts:]
    group = rows * parts
    slots = cap * parts
    me = me_ref[0]
    dim = x_ref.shape[1]
    prim, sec, slot_p = info_ref[0:1, :], info_ref[1:2, :], info_ref[2:3, :]
    place = ((prim >> shift) ^ me) * slots + slot_p
    place = jnp.transpose(jnp.broadcast_to(place.astype(F32), (128, group)))[:, 0:1].astype(I32)
    pick = as_bf(iota((group, parts * slots), 1) == place)
    found = nn(pick, jnp.concatenate([ref[...] for ref in owned], axis=0))
    x = x_ref[...]
    r_ref[...] = (x.astype(F32) - found).astype(BF)
    r = r_ref[...]
    diag = iota((group, group), 0) == iota((group, group), 1)
    rx = jnp.sum(jnp.where(diag, nt(x, r), 0.0), axis=0, keepdims=True)
    rr = jnp.sum(jnp.where(diag, nt(r, r), 0.0), axis=0, keepdims=True)
    spread = rr * (1.0 / dim) + 1e-05
    gain = perpendicular_weighting / (dim * spread)
    sec_row = jnp.where((sec >> shift) == me, sec & ((1 << shift) - 1), -1)

    def first(i, so_far):
        top, picked = so_far
        k = pl.multiple_of(i * tile, tile)
        gap = rx - nt(cent_ref[pl.ds(k, tile), :], r)
        t = (base_ref[pl.ds(k, tile), :] - gain * (gap * gap)) * (1.0 / logit_divisor)
        t_ref[pl.ds(k, tile), :] = t
        hit = (iota((tile, group), 0) + k) == sec_row
        picked = picked + jnp.sum(jnp.where(hit, t, 0.0), axis=0, keepdims=True)
        return jnp.maximum(top, jnp.max(t, axis=0, keepdims=True)), picked

    count = cent_ref.shape[0] // tile
    top, picked = lax.fori_loop(
        0, count, first, (jnp.full((1, group), -jnp.inf, F32), jnp.zeros((1, group), F32))
    )

    def second(i, total):
        k = pl.multiple_of(i * tile, tile)
        e = jnp.exp(t_ref[pl.ds(k, tile), :] - top)
        return total + jnp.sum(e, axis=0, keepdims=True)

    total = lax.fori_loop(0, count, second, jnp.zeros((1, group), F32))
    part = top + jnp.log(total)
    lines = [part[:, i : i + 128] for i in range(0, group, 128)]
    lines += [picked[:, i : i + 128] for i in range(0, group, 128)]
    packed = jnp.concatenate(lines, axis=0)
    out_ref[...] = jnp.broadcast_to(packed[None], out_ref.shape)


def three(a):
    high = a.astype(BF)
    rest = a - high.astype(F32)
    mid = rest.astype(BF)
    return [high, mid, (rest - mid.astype(F32)).astype(BF)]


def lists_kernel(cap, parts, dps, shift, group, tile, me_ref, *refs):
    blocks = refs[:dps]
    cent_ref, sum_ref, diff_ref, hot_ref, lane_ref = refs[dps:]
    slots = cap * parts
    cents = 1 << shift
    width = blocks[0].shape[1]
    at = pl.multiple_of(me_ref[1] * width, width)
    diffs = []
    for s, ref in enumerate(blocks):
        facts = ref[2 * slots :, 0:128].astype(F32)
        valid = facts[0:1, :] > 0.0
        second = iota((1, 128), 1) >= slots
        high = jnp.where(second, facts[10:11, :], facts[8:9, :])
        low = jnp.where(second, facts[11:12, :], facts[9:10, :])
        ids = jnp.where(valid, high * 256.0 + low, -1.0)
        where = jnp.where(valid, facts[1:2, :] * 256.0 + facts[2:3, :], -1.0)
        hot_ref[:, s * 128 : (s + 1) * 128] = as_bf(iota((cents, 128), 0) == ids.astype(I32))
        ids_col = jnp.transpose(jnp.broadcast_to(ids, (128, 128)))[:, 0:1].astype(I32)
        where_col = jnp.transpose(jnp.broadcast_to(where, (128, 128)))[slots:, 0:1].astype(I32)
        lane_ref[s * slots : (s + 1) * slots, :] = jnp.where(
            iota((slots, group), 1) == where_col, 1.0, 0.0
        )
        pick = as_bf(iota((128, cents), 1) == ids_col)
        rows = nn(pick, cent_ref[:, pl.ds(at, width)])
        diff = ref[0 : 2 * slots, :].astype(F32) - rows
        diff_ref[s * slots : (s + 1) * slots, :] = diff[slots:, :]
        diffs.append(jnp.concatenate([diff[0:slots, :], jnp.zeros((slots, width), F32)], axis=0))
    parts3 = three(jnp.concatenate(diffs, axis=0))

    @pl.loop(0, cents, step=tile)
    def _(k):
        k = pl.multiple_of(k, tile)
        hot = hot_ref[pl.ds(k, tile), :]
        sum_ref[pl.ds(k, tile), :] = nn(hot, parts3[0]) + nn(hot, parts3[1]) + nn(hot, parts3[2])


def final_kernel(rows, cap, parts, dps, group, tile, log_count, me_ref, *refs):
    got_ref, sum_ref, diff_ref, hot_ref, lane_ref, cost_ref, out_ref = refs
    slots = cap * parts
    lines = group // 128
    me = me_ref[0]
    terms = []
    for s in range(dps):
        first = (me_ref[1] ^ s) * parts
        part = got_ref[pl.ds(first, parts), 0:lines, :]
        top = jnp.max(part, axis=0)
        lse = top + jnp.log(jnp.sum(jnp.exp(part - top[None]), axis=0))
        if s == 0:
            flat = jnp.concatenate([lse[i : i + 1] for i in range(lines)], axis=1)
            cost = jnp.zeros((1, rows), F32)
            for b in range(parts):
                cost = cost + jnp.where(me == b, flat[:, b * rows : (b + 1) * rows], 0.0)
            cost_ref[...] = cost - log_count
        picked = got_ref[pl.ds(first + me, 1), lines : 2 * lines, :][0]
        z = picked - lse + log_count + spill_offset
        e = jnp.exp(-jnp.abs(z))
        weight = jnp.where(z >= 0.0, 1.0, e) / (1.0 + e)
        weight = jnp.concatenate([weight[i : i + 1] for i in range(lines)], axis=1)
        at = slice(s * slots, (s + 1) * slots)
        column = jnp.sum(lane_ref[at, :] * weight, axis=1, keepdims=True)
        terms.append(jnp.zeros((slots, diff_ref.shape[1]), F32))
        terms.append(column * diff_ref[at, :])
    parts3 = three(jnp.concatenate(terms, axis=0))

    @pl.loop(0, out_ref.shape[0], step=tile)
    def _(k):
        k = pl.multiple_of(k, tile)
        hot = hot_ref[pl.ds(k, tile), :]
        late = nn(hot, parts3[0]) + nn(hot, parts3[1]) + nn(hot, parts3[2])
        out_ref[pl.ds(k, tile), :] = (sum_ref[pl.ds(k, tile), :] + late).astype(BF)


def swap(a, axis, count, step):
    return lax.ppermute(a, axis, [(i, i ^ step) for i in range(count)])


def exchange(a, axis, count):
    blocks = [None] * count
    for s in range(0, count, 2):
        blocks[s] = swap(a, axis, count, s) if s else a
    for s in range(0, count, 2):
        blocks[s + 1] = swap(blocks[s], axis, count, 1)
    return blocks


def per_device(vectors, centroids, primary, secondary):
    rows, dim = vectors.shape
    cents = centroids.shape[0]
    parts = lax.axis_size("cent")
    dps = lax.axis_size("dp")
    group = rows * parts
    cap = 2 * rows // parts
    slots = cap * parts
    shift = cents.bit_length() - 1
    assert cents == 1 << shift and 2 * slots == 128
    width = dim // dps
    tile = 256
    me = jnp.stack([lax.axis_index("cent"), lax.axis_index("dp")]).astype(I32)

    (packed,) = call(
        pack_kernel,
        [((rows + META, dim), BF)],
        [vectors, primary.reshape(1, rows), secondary.reshape(1, rows)],
    )
    blocks = exchange(packed, "cent", parts)
    info, owned = call(
        functools.partial(rows_kernel, rows, cap, parts, shift),
        [((8, group), I32), ((slots, dim), BF)],
        [me, *blocks, centroids],
        smem=1,
    )
    owned = exchange(owned, "cent", parts)
    x_all, *columns = call(
        functools.partial(slots_kernel, rows, cap, parts, dps, shift),
        [((group, dim), BF)] + [((2 * slots + 16, width), BF)] * dps,
        [me, *blocks, info],
        smem=1,
        scratch=[pltpu.VMEM((2 * slots, dim), BF)],
    )
    columns = [columns[0]] + [swap(columns[s], "dp", dps, s) for s in range(1, dps)]
    (base,) = call(
        functools.partial(base_kernel, tile),
        [((cents, group), F32)],
        [x_all, centroids],
    )
    lines = group // 128
    (sent,) = call(
        functools.partial(score_kernel, rows, cap, parts, shift, tile),
        [((dps * parts, 2 * lines, 128), F32)],
        [me, *owned, x_all, info, centroids, base],
        smem=1,
        scratch=[pltpu.VMEM((group, dim), BF), pltpu.VMEM((cents, group), F32)],
        limit=40 * 1024 * 1024,
    )
    got = lax.all_to_all(sent, ("dp", "cent"), 0, 0, tiled=True)
    list_sum, diff, hot, lane = call(
        functools.partial(lists_kernel, cap, parts, dps, shift, group, tile),
        [
            ((cents, width), F32),
            ((dps * slots, width), F32),
            ((cents, dps * 2 * slots), BF),
            ((dps * slots, group), F32),
        ],
        [me, *columns, centroids],
        smem=1,
    )
    log_count = math.log(cents * parts)
    cost, out = call(
        functools.partial(final_kernel, rows, cap, parts, dps, group, tile, log_count),
        [((1, rows), F32), ((cents, width), BF)],
        [me, got, list_sum, diff, hot, lane],
        smem=1,
    )
    return cost.reshape(rows), out


def solution(mesh):
    in_specs = (P(("dp", "cent"), None), P("cent", None), P(("dp", "cent")), P(("dp", "cent")))
    out_specs = (P(("dp", "cent")), P("cent", "dp"))
    return jax.shard_map(
        per_device, mesh=mesh, in_specs=in_specs, out_specs=out_specs, check_vma=False
    )
```

```python
import functools
import math

import jax
import jax.numpy as jnp
from jax import lax
from jax.experimental import pallas as pl
from jax.experimental.pallas import tpu as pltpu
from jax.sharding import PartitionSpec as P

perpendicular_weighting = 1.5
logit_divisor = 40.0
spill_offset = 2.0
BF = jnp.bfloat16
F32 = jnp.float32
I32 = jnp.int32
META = 8
VMEM_LIMIT = 24 * 1024 * 1024


def iota(shape, dim):
    return lax.broadcasted_iota(I32, shape, dim)


def nn(a, b):
    return lax.dot_general(a, b, (((1,), (0,)), ((), ())), preferred_element_type=F32)


def nt(a, b):
    return lax.dot_general(a, b, (((1,), (1,)), ((), ())), preferred_element_type=F32)


def as_bf(mask):
    return jnp.where(mask, 1.0, 0.0).astype(BF)


def call(kernel, outs, args, us=0.0, scratch=(), smem=0, hbm_in=(), hbm_out=(), vmem_in=(), vmem_out=()):
    specs = [pl.BlockSpec(memory_space=pltpu.SMEM)] * smem
    for i in range(smem, len(args)):
        specs.append(pl.BlockSpec(memory_space=pltpu.HBM if i in hbm_in else pltpu.VMEM))
    args = list(args)
    for i in hbm_in:
        args[i] = pltpu.with_memory_space_constraint(args[i], pltpu.HBM)
    for i in vmem_in:
        args[i] = pltpu.with_memory_space_constraint(args[i], pltpu.VMEM)
    return pl.pallas_call(
        kernel,
        out_shape=tuple(
            pltpu.VMEM(s, t) if i in vmem_out else jax.ShapeDtypeStruct(s, t)
            for i, (s, t) in enumerate(outs)
        ),
        in_specs=specs,
        out_specs=tuple(
            pl.BlockSpec(memory_space=pltpu.HBM if i in hbm_out else pltpu.VMEM)
            for i in range(len(outs))
        ),
        scratch_shapes=list(scratch),
        compiler_params=pltpu.CompilerParams(vmem_limit_bytes=VMEM_LIMIT),
        cost_estimate=pl.CostEstimate(
            flops=int(us * 5e8), bytes_accessed=int(us * 2e6), transcendentals=0
        ),
    )(*args)


def pack_kernel(me_ref, x_ref, prim_ref, sec_ref, out_ref, ids_ref, sems):
    rows = x_ref.shape[0]
    copies = [
        pltpu.make_async_copy(prim_ref, ids_ref.at[pl.ds(0, 1)], sems.at[0]),
        pltpu.make_async_copy(sec_ref, ids_ref.at[pl.ds(1, 1)], sems.at[1]),
        pltpu.make_async_copy(x_ref, out_ref.at[pl.ds(0, rows)], sems.at[2]),
    ]
    for copy in copies:
        copy.start()
    out_ref[rows:, 0:128] = jnp.zeros((META, 128), BF)
    for q in range(2):
        copies[q].wait()
        ids = ids_ref[q : q + 1, :]
        at = rows + 2 * q
        out_ref[at : at + 1, 0:rows] = (ids >> 8).astype(F32).astype(BF)
        out_ref[at + 1 : at + 2, 0:rows] = (ids & 255).astype(F32).astype(BF)
    copies[2].wait()


def tiles_in(src_ref, dst_ref, sems, tile, first=0):
    copies = []
    for i in range(dst_ref.shape[0] // tile):
        src = src_ref.at[pl.ds(first + i * tile, tile)]
        copies.append(pltpu.make_async_copy(src, dst_ref.at[pl.ds(i * tile, tile)], sems.at[i]))
    return copies


def load_kernel(tile, cent_ref, out_ref, token_ref, sems):
    copies = tiles_in(cent_ref, out_ref, sems, tile)
    for copy in copies:
        copy.start()
    token_ref[...] = jnp.zeros(token_ref.shape, F32)
    for copy in copies:
        copy.wait()


def rows_kernel(rows, cap, parts, shift, me_ref, *refs):
    blocks = refs[:parts]
    cent_ref, info_ref, out_ref = refs[parts:]
    group = rows * parts
    me = me_ref[0]
    spread = as_bf(iota((128, group), 0) == (iota((128, group), 1) % rows))
    lane_block = iota((META, group), 1) // rows
    bytes8 = jnp.zeros((META, group), F32)
    for s, ref in enumerate(blocks):
        got = nn(ref[rows : rows + META, 0:128], spread)
        bytes8 = bytes8 + jnp.where(lane_block == (me ^ s), got, 0.0)
    bytes8 = bytes8.astype(I32)
    prim = bytes8[0:1] * 256 + bytes8[1:2]
    sec = bytes8[2:3] * 256 + bytes8[3:4]
    before = (iota((group, group), 0) < iota((group, group), 1)) & (
        iota((group, group), 0) // rows == iota((group, group), 1) // rows
    )
    before = as_bf(before)
    ranks = []
    for ids in (prim, sec):
        same = iota((parts, group), 0) == (ids >> shift)
        count = nn(as_bf(same), before)
        ranks.append(jnp.sum(jnp.where(same, count, 0.0), axis=0, keepdims=True).astype(I32))
    base = (iota((1, group), 1) // rows) * cap
    slot_p = base + ranks[0]
    slot_s = base + ranks[1]
    info_ref[0:1, :] = prim
    info_ref[1:2, :] = sec
    info_ref[2:3, :] = slot_p
    info_ref[3:4, :] = slot_s
    info_ref[4:8, :] = jnp.zeros((4, group), I32)
    slots = cap * parts
    keep = (iota((slots, group), 0) == slot_p) & ((prim >> shift) == me)
    local = jnp.where(keep, (prim & ((1 << shift) - 1)) + 1, 0).astype(F32)
    row_id = jnp.sum(local, axis=1, keepdims=True).astype(I32) - 1
    pick = as_bf(iota((slots, 1 << shift), 1) == row_id)
    out_ref[...] = nn(pick, cent_ref[...]).astype(BF)


def slots_kernel(rows, cap, parts, dps, shift, me_ref, *refs):
    blocks = refs[:parts]
    info_ref, x_ref = refs[parts : parts + 2]
    outs = refs[parts + 2 : parts + 2 + dps]
    picked_ref = refs[-1]
    group = rows * parts
    slots = cap * parts
    me = me_ref[0]
    me_dp = me_ref[1]
    for s, ref in enumerate(blocks):
        at = pl.multiple_of((me ^ s) * rows, rows)
        x_ref[pl.ds(at, rows), :] = ref[0:rows, :]
    prim, sec = info_ref[0:1, :], info_ref[1:2, :]
    slot_p, slot_s = info_ref[2:3, :], info_ref[3:4, :]
    keep_p = (iota((slots, group), 0) == slot_p) & ((prim >> shift) == me)
    keep_s = (iota((slots, group), 0) == slot_s) & ((sec >> shift) == me)
    pick = jnp.concatenate([as_bf(keep_p), as_bf(keep_s)], axis=0)
    picked_ref[...] = nn(pick, x_ref[...]).astype(BF)
    where = iota((1, group), 1)
    meta = jnp.concatenate(
        [
            jnp.ones((1, group), F32),
            (where >> 8).astype(F32),
            (where & 255).astype(F32),
            jnp.zeros((5, group), F32),
        ],
        axis=0,
    ).astype(BF)
    mask = (1 << shift) - 1
    local_p, local_s = prim & mask, sec & mask
    loc = jnp.concatenate(
        [
            (local_p >> 8).astype(F32),
            (local_p & 255).astype(F32),
            (local_s >> 8).astype(F32),
            (local_s & 255).astype(F32),
            jnp.zeros((4, group), F32),
        ],
        axis=0,
    ).astype(BF)
    facts = jnp.concatenate([nt(meta, pick), nt(loc, pick)], axis=0).astype(BF)
    width = x_ref.shape[1] // dps
    for s in range(dps):
        at = pl.multiple_of((me_dp ^ s) * width, width)
        outs[s][0 : 2 * slots, :] = picked_ref[:, pl.ds(at, width)]
        outs[s][2 * slots :, 0:128] = facts


def base_kernel(tile, x_ref, cent_ref, out_ref, token_ref):
    x = x_ref[...]
    for k in range(0, cent_ref.shape[0], tile):
        c = cent_ref[k : k + tile, :]
        cf = c.astype(F32)
        out_ref[k : k + tile, :] = 2.0 * nt(c, x) - jnp.sum(cf * cf, axis=1, keepdims=True)
    token_ref[...] = jnp.zeros(token_ref.shape, F32)


def score_kernel(rows, cap, parts, shift, tile, me_ref, *refs):
    owned = refs[:parts]
    x_ref, info_ref, cent_ref, base_ref, out_ref, r_ref, t_ref = refs[parts:]
    group = rows * parts
    slots = cap * parts
    me = me_ref[0]
    dim = x_ref.shape[1]
    prim, sec, slot_p = info_ref[0:1, :], info_ref[1:2, :], info_ref[2:3, :]
    place = ((prim >> shift) ^ me) * slots + slot_p
    place = jnp.transpose(jnp.broadcast_to(place.astype(F32), (128, group)))[:, 0:1].astype(I32)
    pick = as_bf(iota((group, parts * slots), 1) == place)
    found = nn(pick, jnp.concatenate([ref[...] for ref in owned], axis=0))
    x = x_ref[...]
    r_ref[...] = (x.astype(F32) - found).astype(BF)
    r = r_ref[...]
    diag = iota((group, group), 0) == iota((group, group), 1)
    rx = jnp.sum(jnp.where(diag, nt(x, r), 0.0), axis=0, keepdims=True)
    rr = jnp.sum(jnp.where(diag, nt(r, r), 0.0), axis=0, keepdims=True)
    spread = rr * (1.0 / dim) + 1e-05
    gain = perpendicular_weighting / (dim * spread)
    sec_row = jnp.where((sec >> shift) == me, sec & ((1 << shift) - 1), -1)

    top = jnp.full((1, group), -jnp.inf, F32)
    picked = jnp.zeros((1, group), F32)
    count = cent_ref.shape[0] // tile
    for i in range(count):
        at = slice(i * tile, (i + 1) * tile)
        gap = rx - nt(cent_ref[at, :], r)
        t = (base_ref[at, :] - gain * (gap * gap)) * (1.0 / logit_divisor)
        t_ref[at, :] = t
        hit = (iota((tile, group), 0) + i * tile) == sec_row
        picked = picked + jnp.sum(jnp.where(hit, t, 0.0), axis=0, keepdims=True)
        top = jnp.maximum(top, jnp.max(t, axis=0, keepdims=True))

    total = jnp.zeros((1, group), F32)
    for i in range(count):
        e = jnp.exp(t_ref[i * tile : (i + 1) * tile, :] - top)
        total = total + jnp.sum(e, axis=0, keepdims=True)
    part = top + jnp.log(total)
    lines = [part[:, i : i + 128] for i in range(0, group, 128)]
    lines += [picked[:, i : i + 128] for i in range(0, group, 128)]
    packed = jnp.concatenate(lines, axis=0)
    out_ref[...] = jnp.broadcast_to(packed[None], out_ref.shape)


def split(a):
    high = a.astype(BF)
    return high, (a - high.astype(F32)).astype(BF)


def lists_kernel(cap, parts, dps, shift, group, tile, me_ref, *refs):
    blocks = refs[:dps]
    cent_ref, sum_ref, diff_ref, ids_ref, lane_ref, c_ref, blocks_ref, sems = refs[dps:]
    slots = cap * parts
    cents = 1 << shift
    width = blocks[0].shape[1]
    at = pl.multiple_of(me_ref[1] * width, width)
    copies = [pltpu.make_async_copy(cent_ref.at[:, pl.ds(at, width)], c_ref, sems.at[0])]
    for s in range(1, dps):
        copies.append(pltpu.make_async_copy(blocks[s], blocks_ref.at[s - 1], sems.at[s]))
    for copy in copies:
        copy.start()
    for copy in copies:
        copy.wait()
    diffs, ids_p, ids_s = [], [], []
    for s in range(dps):
        ref = blocks_ref.at[s - 1] if s else blocks[0]
        facts = ref[2 * slots :, 0:128].astype(F32)
        valid = facts[0:1, :] > 0.0
        second = iota((1, 128), 1) >= slots
        high = jnp.where(second, facts[10:11, :], facts[8:9, :])
        low = jnp.where(second, facts[11:12, :], facts[9:10, :])
        ids = jnp.where(valid, high * 256.0 + low, -1.0)
        where = jnp.where(valid, facts[1:2, :] * 256.0 + facts[2:3, :], -1.0)
        ids_p.append(ids[:, 0:slots])
        ids_s.append(ids[:, slots : 2 * slots])
        ids_col = jnp.transpose(jnp.broadcast_to(ids, (128, 128)))[:, 0:1].astype(I32)
        where_col = jnp.transpose(jnp.broadcast_to(where, (128, 128)))[slots:, 0:1].astype(I32)
        lane_ref[s * slots : (s + 1) * slots, :] = as_bf(
            iota((slots, group), 1) == where_col
        )
        pick = as_bf(iota((128, cents), 1) == ids_col)
        rows = nn(pick, c_ref[...])
        diff = ref[0 : 2 * slots, :].astype(F32) - rows
        diff_ref[s * slots : (s + 1) * slots, :] = diff[slots:, :]
        diffs.append(diff[0:slots, :])
    high, low = split(jnp.concatenate(diffs, axis=0))
    ids_p = jnp.concatenate(ids_p, axis=1).astype(I32)
    ids_s = jnp.concatenate(ids_s, axis=1).astype(I32)
    ids_ref[...] = jnp.broadcast_to(ids_s, ids_ref.shape)

    @pl.loop(0, cents, step=tile)
    def _(k):
        k = pl.multiple_of(k, tile)
        hot = as_bf((iota((tile, dps * slots), 0) + k) == ids_p)
        sum_ref[pl.ds(k, tile), :] = nn(hot, high) + nn(hot, low)


def final_kernel(rows, cap, parts, dps, group, tile, log_count, me_ref, *refs):
    got_ref, sum_ref, diff_ref, ids_ref, lane_ref, cost_ref, out_ref, weight_ref, part_ref, sems = refs
    slots = cap * parts
    lines = group // 128
    me = me_ref[0]
    part = got_ref[:, 0:lines, :].reshape(dps, parts, lines, 128)
    top = jnp.max(part, axis=1)
    lse = top + jnp.log(jnp.sum(jnp.exp(part - top[:, None]), axis=1))
    picked = jnp.concatenate(
        [got_ref[pl.ds(d * parts + me, 1), lines : 2 * lines, :] for d in range(dps)], axis=0
    )
    z = picked - lse + log_count + spill_offset
    e = jnp.exp(-jnp.abs(z))
    weight = jnp.where(z >= 0.0, 1.0, e) / (1.0 + e)
    for d in range(dps):
        for i in range(lines):
            at = slice(i * 128, (i + 1) * 128)
            weight_ref[d : d + 1, at] = weight[d, i : i + 1, :]
            weight_ref[dps + d : dps + d + 1, at] = lse[d, i : i + 1, :]
    terms = []
    for s in range(dps):
        at = slice(s * slots, (s + 1) * slots)
        mine = weight_ref[pl.ds(me_ref[1] ^ s, 1), :]
        column = jnp.sum(lane_ref[at, :].astype(F32) * mine, axis=1, keepdims=True)
        terms.append(column * diff_ref[at, :])
    high, low = split(jnp.concatenate(terms, axis=0))
    ids = ids_ref[0:1, :]
    count = out_ref.shape[0] // tile
    copies = []
    for i in range(count):
        at = pl.ds(i * tile, tile)
        hot = as_bf((iota((tile, dps * slots), 0) + i * tile) == ids)
        part_ref[at, :] = (sum_ref[at, :] + (nn(hot, high) + nn(hot, low))).astype(BF)
        copies.append(pltpu.make_async_copy(part_ref.at[at], out_ref.at[at], sems.at[i]))
        copies[i].start()
    flat = weight_ref[pl.ds(dps + me_ref[1], 1), :]
    cost = jnp.zeros((1, rows), F32)
    for b in range(parts):
        cost = cost + jnp.where(me == b, flat[:, b * rows : (b + 1) * rows], 0.0)
    cost_ref[...] = cost - log_count
    for copy in copies:
        copy.wait()


def swap(a, axis, count, step):
    return lax.ppermute(a, axis, [(i, i ^ step) for i in range(count)])


def after(a, token):
    return lax.optimization_barrier((a, token))[0]


def far_blocks(a, count):
    return [a] + [swap(a, "cent", count, s) for s in range(2, count, 2)]


def all_blocks(far, token, count):
    near = [swap(far[0], "cent", count, 1)]
    near += [swap(after(a, token), "cent", count, 1) for a in far[1:]]
    return [a for pair in zip(far, near) for a in pair]


def per_device(vectors, centroids, primary, secondary):
    rows, dim = vectors.shape
    cents = centroids.shape[0]
    parts = lax.axis_size("cent")
    dps = lax.axis_size("dp")
    group = rows * parts
    cap = 2 * rows // parts
    slots = cap * parts
    shift = cents.bit_length() - 1
    assert cents == 1 << shift and 2 * slots == 128
    width = dim // dps
    tile = 256
    lines = group // 128
    token_out = ((8, 128), F32)
    me = jnp.stack([lax.axis_index("cent"), lax.axis_index("dp")]).astype(I32)

    (packed,) = call(
        pack_kernel,
        [((rows + META, dim), BF)],
        [me, vectors, primary.reshape(1, rows), secondary.reshape(1, rows)],
        smem=1,
        hbm_in=(1, 2, 3),
        scratch=[pltpu.VMEM((2, rows), I32), pltpu.SemaphoreType.DMA((3,))],
    )
    packed, cent = lax.optimization_barrier((packed, centroids))
    far = far_blocks(packed, parts)
    cent, token = call(
        functools.partial(load_kernel, tile),
        [((cents, dim), BF), token_out],
        [cent],
        us=3.0,
        hbm_in=(0,),
        vmem_out=(0,),
        scratch=[pltpu.SemaphoreType.DMA((cents // tile,))],
    )
    blocks = all_blocks(far, token, parts)
    info, owned = call(
        functools.partial(rows_kernel, rows, cap, parts, shift),
        [((8, group), I32), ((slots, dim), BF)],
        [me, *blocks, cent],
        us=2.0,
        smem=1,
        vmem_in=(parts + 1,),
    )
    far = far_blocks(owned, parts)
    x_all, *columns = call(
        functools.partial(slots_kernel, rows, cap, parts, dps, shift),
        [((group, dim), BF)] + [((2 * slots + 16, width), BF)] * dps,
        [me, *blocks, info],
        us=1.0,
        smem=1,
        scratch=[pltpu.VMEM((2 * slots, dim), BF)],
    )
    columns = [columns[0]] + [swap(columns[s], "dp", dps, s) for s in range(1, dps)]
    base, token = call(
        functools.partial(base_kernel, tile),
        [((cents, group), F32), token_out],
        [x_all, cent],
        us=2.0,
        vmem_in=(1,),
    )
    owned = all_blocks(far, token, parts)
    (sent,) = call(
        functools.partial(score_kernel, rows, cap, parts, shift, tile),
        [((dps * parts, 2 * lines, 128), F32)],
        [me, *owned, x_all, info, cent, base],
        us=6.0,
        smem=1,
        vmem_in=(parts + 3,),
        scratch=[pltpu.VMEM((group, dim), BF), pltpu.VMEM((cents, group), F32)],
    )
    sent, columns[0] = lax.optimization_barrier((sent, columns[0]))
    got = lax.all_to_all(sent, ("dp", "cent"), 0, 0, tiled=True)
    list_sum, diff, ids, lane = call(
        functools.partial(lists_kernel, cap, parts, dps, shift, group, tile),
        [
            ((cents, width), F32),
            ((dps * slots, width), F32),
            ((8, dps * slots), I32),
            ((dps * slots, group), BF),
        ],
        [me, *columns, centroids],
        smem=1,
        hbm_in=tuple(range(2, dps + 2)),
        us=4.0,
        scratch=[
            pltpu.VMEM((cents, width), BF),
            pltpu.VMEM((dps - 1, 2 * slots + 16, width), BF),
            pltpu.SemaphoreType.DMA((dps,)),
        ],
    )
    log_count = math.log(cents * parts)
    cost, out = call(
        functools.partial(final_kernel, rows, cap, parts, dps, group, tile, log_count),
        [((1, rows), F32), ((cents, width), BF)],
        [me, got, list_sum, diff, ids, lane],
        smem=1,
        hbm_out=(1,),
        scratch=[
            pltpu.VMEM((2 * dps, group), F32),
            pltpu.VMEM((cents, width), BF),
            pltpu.SemaphoreType.DMA((cents // tile,)),
        ],
    )
    return cost.reshape(rows), out


def solution(mesh):
    in_specs = (P(("dp", "cent"), None), P("cent", None), P(("dp", "cent")), P(("dp", "cent")))
    out_specs = (P(("dp", "cent")), P("cent", "dp"))
    return jax.shard_map(
        per_device, mesh=mesh, in_specs=in_specs, out_specs=out_specs, check_vma=False
    )
```

```python
import functools
import math

import jax
import jax.numpy as jnp
from jax import lax
from jax.experimental import pallas as pl
from jax.experimental.pallas import tpu as pltpu
from jax.sharding import PartitionSpec as P

perpendicular_weighting = 1.5
logit_divisor = 40.0
spill_offset = 2.0
BF = jnp.bfloat16
F32 = jnp.float32
I32 = jnp.int32
META = 8
VMEM_LIMIT = 24 * 1024 * 1024


def iota(shape, dim):
    return lax.broadcasted_iota(I32, shape, dim)


def nn(a, b):
    return lax.dot_general(a, b, (((1,), (0,)), ((), ())), preferred_element_type=F32)


def nt(a, b):
    return lax.dot_general(a, b, (((1,), (1,)), ((), ())), preferred_element_type=F32)


def as_bf(mask):
    return jnp.where(mask, 1.0, 0.0).astype(BF)


def here():
    return lax.axis_index("cent"), lax.axis_index("dp")


def call(kernel, outs, args, us=0.0, scratch=(), smem=0, hbm_in=(), hbm_out=(), vmem_in=(), vmem_out=()):
    specs = [pl.BlockSpec(memory_space=pltpu.SMEM)] * smem
    for i in range(smem, len(args)):
        specs.append(pl.BlockSpec(memory_space=pltpu.HBM if i in hbm_in else pltpu.VMEM))
    args = list(args)
    for i in hbm_in:
        args[i] = pltpu.with_memory_space_constraint(args[i], pltpu.HBM)
    for i in vmem_in:
        args[i] = pltpu.with_memory_space_constraint(args[i], pltpu.VMEM)
    return pl.pallas_call(
        kernel,
        out_shape=tuple(
            pltpu.VMEM(s, t) if i in vmem_out else jax.ShapeDtypeStruct(s, t)
            for i, (s, t) in enumerate(outs)
        ),
        in_specs=specs,
        out_specs=tuple(
            pl.BlockSpec(memory_space=pltpu.HBM if i in hbm_out else pltpu.VMEM)
            for i in range(len(outs))
        ),
        scratch_shapes=list(scratch),
        compiler_params=pltpu.CompilerParams(vmem_limit_bytes=VMEM_LIMIT),
        cost_estimate=pl.CostEstimate(
            flops=int(us * 5e8), bytes_accessed=int(us * 2e6), transcendentals=0
        ),
    )(*args)


def pack_kernel(x_ref, prim_ref, sec_ref, out_ref, ids_ref, sems):
    rows = x_ref.shape[0]
    copies = [
        pltpu.make_async_copy(prim_ref, ids_ref.at[pl.ds(0, 1)], sems.at[0]),
        pltpu.make_async_copy(sec_ref, ids_ref.at[pl.ds(1, 1)], sems.at[1]),
        pltpu.make_async_copy(x_ref, out_ref.at[pl.ds(0, rows)], sems.at[2]),
    ]
    for copy in copies:
        copy.start()
    out_ref[rows:, 0:128] = jnp.zeros((META, 128), BF)
    for q in range(2):
        copies[q].wait()
        ids = ids_ref[q : q + 1, :]
        at = rows + 2 * q
        out_ref[at : at + 1, 0:rows] = (ids >> 8).astype(F32).astype(BF)
        out_ref[at + 1 : at + 2, 0:rows] = (ids & 255).astype(F32).astype(BF)
    copies[2].wait()


def tiles_in(src_ref, dst_ref, sems, tile, first=0):
    copies = []
    for i in range(dst_ref.shape[0] // tile):
        src = src_ref.at[pl.ds(first + i * tile, tile)]
        copies.append(pltpu.make_async_copy(src, dst_ref.at[pl.ds(i * tile, tile)], sems.at[i]))
    return copies


def load_kernel(tile, cent_ref, out_ref, token_ref, sems):
    copies = tiles_in(cent_ref, out_ref, sems, tile)
    for copy in copies:
        copy.start()
    token_ref[...] = jnp.zeros(token_ref.shape, F32)
    for copy in copies:
        copy.wait()


def slots_of(ids, rows, cap, parts, shift):
    group = rows * parts
    row, lane = iota((group, group), 0), iota((group, group), 1)
    before = as_bf((row < lane) & (row // rows == lane // rows))
    same = iota((parts, group), 0) == (ids >> shift)
    count = nn(as_bf(same), before)
    rank = jnp.sum(jnp.where(same, count, 0.0), axis=0, keepdims=True).astype(I32)
    return (iota((1, group), 1) // rows) * cap + rank


def rows_kernel(rows, cap, parts, shift, *refs):
    blocks = refs[:parts]
    cent_ref, info_ref, out_ref = refs[parts:]
    group = rows * parts
    me, me_dp = here()
    spread = as_bf(iota((128, group), 0) == (iota((128, group), 1) % rows))
    lane_block = iota((META, group), 1) // rows
    got = nn(jnp.concatenate([ref[rows : rows + META, 0:128] for ref in blocks], axis=0), spread)
    bytes8 = jnp.zeros((META, group), F32)
    for s in range(parts):
        at = slice(s * META, (s + 1) * META)
        bytes8 = bytes8 + jnp.where(lane_block == (me ^ s), got[at, :], 0.0)
    bytes8 = bytes8.astype(I32)
    prim = bytes8[0:1] * 256 + bytes8[1:2]
    sec = bytes8[2:3] * 256 + bytes8[3:4]
    slot_p = slots_of(prim, rows, cap, parts, shift)
    info_ref[0:1, :] = prim
    info_ref[1:2, :] = sec
    info_ref[2:3, :] = slot_p
    info_ref[3:8, :] = jnp.zeros((5, group), I32)
    slots = cap * parts
    keep = (iota((slots, group), 0) == slot_p) & ((prim >> shift) == me)
    local = jnp.where(keep, (prim & ((1 << shift) - 1)) + 1, 0).astype(F32)
    row_id = jnp.sum(local, axis=1, keepdims=True).astype(I32) - 1
    pick = as_bf(iota((slots, 1 << shift), 1) == row_id)
    out_ref[...] = nn(pick, cent_ref[...]).astype(BF)


def slots_kernel(rows, cap, parts, dps, shift, *refs):
    blocks = refs[:parts]
    info_ref, x_ref = refs[parts : parts + 2]
    out_ref, picked_ref = refs[parts + 2 :]
    group = rows * parts
    slots = cap * parts
    me, me_dp = here()
    for s, ref in enumerate(blocks):
        at = pl.multiple_of((me ^ s) * rows, rows)
        x_ref[pl.ds(at, rows), :] = ref[0:rows, :]
    prim, sec = info_ref[0:1, :], info_ref[1:2, :]
    slot_p, slot_s = info_ref[2:3, :], slots_of(sec, rows, cap, parts, shift)
    keep_p = (iota((slots, group), 0) == slot_p) & ((prim >> shift) == me)
    keep_s = (iota((slots, group), 0) == slot_s) & ((sec >> shift) == me)
    pick = jnp.concatenate([as_bf(keep_p), as_bf(keep_s)], axis=0)
    picked_ref[...] = nn(pick, x_ref[...]).astype(BF)
    where = iota((1, group), 1)
    meta = jnp.concatenate(
        [
            jnp.ones((1, group), F32),
            (where >> 8).astype(F32),
            (where & 255).astype(F32),
            jnp.zeros((5, group), F32),
        ],
        axis=0,
    ).astype(BF)
    mask = (1 << shift) - 1
    local_p, local_s = prim & mask, sec & mask
    loc = jnp.concatenate(
        [
            (local_p >> 8).astype(F32),
            (local_p & 255).astype(F32),
            (local_s >> 8).astype(F32),
            (local_s & 255).astype(F32),
            jnp.zeros((4, group), F32),
        ],
        axis=0,
    ).astype(BF)
    facts = jnp.concatenate([nt(meta, pick), nt(loc, pick)], axis=0).astype(BF)
    width = x_ref.shape[1] // dps
    for s in range(dps):
        out_ref[s, 0 : 2 * slots, :] = picked_ref[:, s * width : (s + 1) * width]
        out_ref[s, 2 * slots :, 0:128] = facts


def base_kernel(tile, x_ref, cent_ref, out_ref, token_ref):
    x = x_ref[...]
    for k in range(0, cent_ref.shape[0], tile):
        c = cent_ref[k : k + tile, :]
        cf = c.astype(F32)
        out_ref[k : k + tile, :] = 2.0 * nt(c, x) - jnp.sum(cf * cf, axis=1, keepdims=True)
    token_ref[...] = jnp.zeros(token_ref.shape, F32)


def score_kernel(rows, cap, parts, shift, tile, *refs):
    owned = refs[:parts]
    x_ref, info_ref, cent_ref, base_ref, out_ref, r_ref, t_ref = refs[parts:]
    group = rows * parts
    slots = cap * parts
    me, me_dp = here()
    dim = x_ref.shape[1]
    prim, sec, slot_p = info_ref[0:1, :], info_ref[1:2, :], info_ref[2:3, :]
    place = ((prim >> shift) ^ me) * slots + slot_p
    place = jnp.transpose(jnp.broadcast_to(place.astype(F32), (128, group)))[:, 0:1].astype(I32)
    pick = as_bf(iota((group, parts * slots), 1) == place)
    found = nn(pick, jnp.concatenate([ref[...] for ref in owned], axis=0))
    x = x_ref[...]
    r_ref[...] = (x.astype(F32) - found).astype(BF)
    r = r_ref[...]
    diag = iota((group, group), 0) == iota((group, group), 1)
    rx = jnp.sum(jnp.where(diag, nt(x, r), 0.0), axis=0, keepdims=True)
    rr = jnp.sum(jnp.where(diag, nt(r, r), 0.0), axis=0, keepdims=True)
    spread = rr * (1.0 / dim) + 1e-05
    gain = perpendicular_weighting / (dim * spread)
    sec_row = jnp.where((sec >> shift) == me, sec & ((1 << shift) - 1), -1)

    top = jnp.full((1, group), -jnp.inf, F32)
    picked = jnp.zeros((1, group), F32)
    count = cent_ref.shape[0] // tile
    for i in range(count):
        at = slice(i * tile, (i + 1) * tile)
        gap = rx - nt(cent_ref[at, :], r)
        t = (base_ref[at, :] - gain * (gap * gap)) * (1.0 / logit_divisor)
        t_ref[at, :] = t
        hit = (iota((tile, group), 0) + i * tile) == sec_row
        picked = picked + jnp.sum(jnp.where(hit, t, 0.0), axis=0, keepdims=True)
        top = jnp.maximum(top, jnp.max(t, axis=0, keepdims=True))

    total = jnp.zeros((1, group), F32)
    for i in range(count):
        e = jnp.exp(t_ref[i * tile : (i + 1) * tile, :] - top)
        total = total + jnp.sum(e, axis=0, keepdims=True)
    part = top + jnp.log(total)
    lines = [part[:, i : i + 128] for i in range(0, group, 128)]
    lines += [picked[:, i : i + 128] for i in range(0, group, 128)]
    packed = jnp.concatenate(lines, axis=0)
    out_ref[...] = jnp.broadcast_to(packed[None], out_ref.shape)


def split(a):
    high = a.astype(BF)
    return high, (a - high.astype(F32)).astype(BF)


def lists_kernel(cap, parts, dps, shift, group, tile, *refs):
    blocks_ref, cent_ref, sum_ref, diff_ref, ids_ref, lane_ref, c_ref, sem = refs
    blocks = [blocks_ref.at[s] for s in range(dps)]
    slots = cap * parts
    cents = 1 << shift
    width = blocks[0].shape[1]
    at = pl.multiple_of(here()[1] * width, width)
    copy = pltpu.make_async_copy(cent_ref.at[:, pl.ds(at, width)], c_ref, sem)
    copy.start()
    picks, ids_p, ids_s = [], [], []
    second = iota((1, 128), 1) >= slots
    for s, ref in enumerate(blocks):
        facts = ref[2 * slots :, 0:128].astype(F32)
        valid = facts[0:1, :] > 0.0
        high = jnp.where(second, facts[10:11, :], facts[8:9, :])
        low = jnp.where(second, facts[11:12, :], facts[9:10, :])
        ids = jnp.where(valid, high * 256.0 + low, -1.0)
        where = jnp.where(valid, facts[1:2, :] * 256.0 + facts[2:3, :], -1.0)
        ids_p.append(ids[:, 0:slots])
        ids_s.append(ids[:, slots : 2 * slots])
        ids_col = jnp.transpose(jnp.broadcast_to(ids, (128, 128)))[:, 0:1].astype(I32)
        where_col = jnp.transpose(jnp.broadcast_to(where, (128, 128)))[slots:, 0:1].astype(I32)
        lane_ref[s * slots : (s + 1) * slots, :] = as_bf(iota((slots, group), 1) == where_col)
        picks.append(as_bf(iota((128, cents), 1) == ids_col))
    ids_p = jnp.concatenate(ids_p, axis=1).astype(I32)
    ids_s = jnp.concatenate(ids_s, axis=1).astype(I32)
    ids_ref[...] = jnp.broadcast_to(ids_s, ids_ref.shape)
    copy.wait()
    rows = nn(jnp.concatenate(picks, axis=0), c_ref[...])
    diffs = []
    for s, ref in enumerate(blocks):
        diff = ref[0 : 2 * slots, :].astype(F32) - rows[s * 128 : (s + 1) * 128, :]
        diff_ref[s * slots : (s + 1) * slots, :] = diff[slots:, :]
        diffs.append(diff[0:slots, :])
    high, low = split(jnp.concatenate(diffs, axis=0))
    for k in range(0, cents, tile):
        hot = as_bf((iota((tile, dps * slots), 0) + k) == ids_p)
        sum_ref[k : k + tile, :] = nn(hot, high) + nn(hot, low)


def final_kernel(rows, cap, parts, dps, group, tile, log_count, *refs):
    got_ref, sum_ref, diff_ref, ids_ref, lane_ref, cost_ref, out_ref, weight_ref, part_ref, sems = refs
    slots = cap * parts
    lines = group // 128
    me, me_dp = here()
    part = got_ref[:, 0:lines, :].reshape(dps, parts, lines, 128)
    top = jnp.max(part, axis=1)
    lse = top + jnp.log(jnp.sum(jnp.exp(part - top[:, None]), axis=1))
    picked = jnp.concatenate(
        [got_ref[pl.ds(d * parts + me, 1), lines : 2 * lines, :] for d in range(dps)], axis=0
    )
    z = picked - lse + log_count + spill_offset
    e = jnp.exp(-jnp.abs(z))
    weight = jnp.where(z >= 0.0, 1.0, e) / (1.0 + e)
    for d in range(dps):
        for i in range(lines):
            at = slice(i * 128, (i + 1) * 128)
            weight_ref[d : d + 1, at] = weight[d, i : i + 1, :]
            weight_ref[dps + d : dps + d + 1, at] = lse[d, i : i + 1, :]
    terms = []
    for s in range(dps):
        at = slice(s * slots, (s + 1) * slots)
        mine = weight_ref[s : s + 1, :]
        column = jnp.sum(lane_ref[at, :].astype(F32) * mine, axis=1, keepdims=True)
        terms.append(column * diff_ref[at, :])
    high, low = split(jnp.concatenate(terms, axis=0))
    ids = ids_ref[0:1, :]
    count = out_ref.shape[0] // tile
    copies = []
    for i in range(count):
        at = pl.ds(i * tile, tile)
        hot = as_bf((iota((tile, dps * slots), 0) + i * tile) == ids)
        part_ref[at, :] = (sum_ref[at, :] + (nn(hot, high) + nn(hot, low))).astype(BF)
        copies.append(pltpu.make_async_copy(part_ref.at[at], out_ref.at[at], sems.at[i]))
        copies[i].start()
    flat = weight_ref[pl.ds(dps + me_dp, 1), :]
    cost = jnp.zeros((1, rows), F32)
    for b in range(parts):
        cost = cost + jnp.where(me == b, flat[:, b * rows : (b + 1) * rows], 0.0)
    cost_ref[...] = cost - log_count
    for copy in copies:
        copy.wait()


def swap(a, axis, count, step):
    return lax.ppermute(a, axis, [(i, i ^ step) for i in range(count)])


def after(a, token):
    return lax.optimization_barrier((a, token))[0]


def far_blocks(a, count):
    return [a] + [swap(a, "cent", count, s) for s in range(2, count, 2)]


def all_blocks(far, token, count):
    near = [swap(after(a, token), "cent", count, 1) for a in far]
    return [a for pair in zip(far, near) for a in pair]


def per_device(vectors, centroids, primary, secondary):
    rows, dim = vectors.shape
    cents = centroids.shape[0]
    parts = lax.axis_size("cent")
    dps = lax.axis_size("dp")
    group = rows * parts
    cap = 2 * rows // parts
    slots = cap * parts
    shift = cents.bit_length() - 1
    assert cents == 1 << shift and 2 * slots == 128
    width = dim // dps
    tile = 256
    lines = group // 128
    token_out = ((8, 128), F32)

    (packed,) = call(
        pack_kernel,
        [((rows + META, dim), BF)],
        [vectors, primary.reshape(1, rows), secondary.reshape(1, rows)],
        hbm_in=(0, 1, 2),
        scratch=[pltpu.VMEM((2, rows), I32), pltpu.SemaphoreType.DMA((3,))],
    )
    packed, cent = lax.optimization_barrier((packed, centroids))
    far = far_blocks(packed, parts)
    cent, token = call(
        functools.partial(load_kernel, tile),
        [((cents, dim), BF), token_out],
        [cent],
        us=3.0,
        hbm_in=(0,),
        vmem_out=(0,),
        scratch=[pltpu.SemaphoreType.DMA((cents // tile,))],
    )
    blocks = all_blocks(far, token, parts)
    info, owned = call(
        functools.partial(rows_kernel, rows, cap, parts, shift),
        [((8, group), I32), ((slots, dim), BF)],
        [*blocks, cent],
        us=2.0,
        vmem_in=(parts,),
    )
    far = far_blocks(owned, parts)
    x_all, columns = call(
        functools.partial(slots_kernel, rows, cap, parts, dps, shift),
        [((group, dim), BF), ((dps, 2 * slots + 16, width), BF)],
        [*blocks, info],
        us=1.0,
        scratch=[pltpu.VMEM((2 * slots, dim), BF)],
    )
    columns = lax.all_to_all(columns, "dp", 0, 0, tiled=True)
    base, token = call(
        functools.partial(base_kernel, tile),
        [((cents, group), F32), token_out],
        [x_all, cent],
        us=2.0,
        vmem_in=(1,),
    )
    owned = all_blocks(far, token, parts)
    owned[0], columns = lax.optimization_barrier((owned[0], columns))
    (sent,) = call(
        functools.partial(score_kernel, rows, cap, parts, shift, tile),
        [((dps * parts, 2 * lines, 128), F32)],
        [*owned, x_all, info, cent, base],
        us=6.0,
        vmem_in=(parts + 2,),
        scratch=[pltpu.VMEM((group, dim), BF), pltpu.VMEM((cents, group), F32)],
    )
    columns = after(columns, sent)
    got = lax.all_to_all(sent, ("dp", "cent"), 0, 0, tiled=True)
    list_sum, diff, ids, lane = call(
        functools.partial(lists_kernel, cap, parts, dps, shift, group, tile),
        [
            ((cents, width), F32),
            ((dps * slots, width), F32),
            ((8, dps * slots), I32),
            ((dps * slots, group), BF),
        ],
        [columns, centroids],
        hbm_in=(1,),
        vmem_in=(0,),
        us=4.0,
        scratch=[
            pltpu.VMEM((cents, width), BF),
            pltpu.SemaphoreType.DMA,
        ],
    )
    log_count = math.log(cents * parts)
    cost, out = call(
        functools.partial(final_kernel, rows, cap, parts, dps, group, tile, log_count),
        [((1, rows), F32), ((cents, width), BF)],
        [got, list_sum, diff, ids, lane],
        hbm_out=(1,),
        scratch=[
            pltpu.VMEM((2 * dps, group), F32),
            pltpu.VMEM((cents, width), BF),
            pltpu.SemaphoreType.DMA((cents // tile,)),
        ],
    )
    return cost.reshape(rows), out


def solution(mesh):
    in_specs = (P(("dp", "cent"), None), P("cent", None), P(("dp", "cent")), P(("dp", "cent")))
    out_specs = (P(("dp", "cent")), P("cent", "dp"))
    return jax.shard_map(
        per_device, mesh=mesh, in_specs=in_specs, out_specs=out_specs, check_vma=False
    )
```
